32 devices in a mesh: aux: 4 (over y, x), blk: 8 (over z, core).
Axes of the slice: x: 2, y: 2, z: 4, core: 2. Of those that a mesh axis runs over, the one named last changes fastest.
Arguments:
- three_center: bfloat16 [384, 4, 128, 128], P(('aux', 'blk')), may hold values from -6 to 6
- slot_block: int32 [384], P(('aux', 'blk')), may hold values from 0 to 47
- slot_aux: int32 [384], P(('aux', 'blk')), may hold values from 0 to 1
- live_slots: int32 [32], P(('aux', 'blk')), may hold values from 1 to 12, as said below
- vir_coef: bfloat16 [6144, 256], replicated, may hold values from -0.00478416 to 0.00478416
- eps_occ: float32 [4000], replicated, may hold values from -1.5 to -0.3
- eps_vir: float32 [256], replicated, may hold values from 0.2 to 3
- occ_index: int32 [4], replicated, may hold values from 0 to 3999, as said below
Outputs:
- amplitudes: float32 [4, 256, 4, 256], P('aux', 'blk')
- pair_energy: float32 [4, 4], P('aux')
The draws below stay inside these ranges and needn't reach their ends.
Inputs may be any that keep to these rules, and one draw needn't show every extreme that they name: The slots in use on a device are its first live_slots ones; the others hold data that is not used. Some device holds exactly 12 slots in use in every draw. `occ_index`: the indices are distinct; the first and the last occupied orbital of the system are in every batch.
All inputs are finite; a program needn't handle non-finite values.
Results may differ from the reference program's by a relative error of at most 0.0035.
Values may be sent and summed in bfloat16 or wider, within the bound.
A program may use at most 64 MiB of HBM per device.

```python
import jax
import jax.numpy as jnp
from jax import lax

VIRTUAL = 256
AO_BLOCK = 128
AUX_BLOCK = 128
AUX_BLOCKS_DEV = 2
SLOT_DEV = 12
AO_BLOCKS = 48
OCC_ALL = 4000
DEVICE_COUNT = 32
OCC_BATCH = 4
AUX_TOTAL = 8192
SLOT_ALL = 384


def sample_values(key, shape, limit):
    return jnp.clip(jax.random.normal(key, shape, jnp.float32), -limit, limit)


def draw_three_center(key, part):
    offsets = jax.random.randint(jax.random.fold_in(key, 3), (OCC_BATCH,), 1, AO_BLOCK)
    places = (jnp.arange(AO_BLOCK)[None, :] + offsets[:, None]) % AO_BLOCK
    pair_weight = 0.35 ** 0.5
    own_weight = 0.3 ** 0.5
    key_shared = jax.random.fold_in(key, 41)
    key_own = jax.random.fold_in(key, 43)

    def one_slot(slot_id):
        shared = sample_values(jax.random.fold_in(key_shared, slot_id), (AUX_BLOCK, AO_BLOCK), 3.45)
        own_part = sample_values(jax.random.fold_in(key_own, slot_id), (OCC_BATCH, AUX_BLOCK, AO_BLOCK), 3.45)
        rolled = jnp.transpose(jnp.take(shared, places, axis=1), (1, 0, 2))
        mixed = pair_weight * (shared[None] + rolled) + own_weight * own_part
        return mixed.astype(jnp.bfloat16)
    return lax.map(one_slot, jnp.arange(SLOT_ALL))


def draw_vir_coef(key, part):
    scale_factor = (AO_BLOCK * AUX_TOTAL * 1.5) ** (-0.5)
    common_weight = 0.35 ** 0.5
    own_weight = 0.65 ** 0.5
    common = sample_values(jax.random.fold_in(key, 51), (AO_BLOCK, VIRTUAL), 4.29)
    own_part = sample_values(jax.random.fold_in(key, 53), (AO_BLOCKS * AO_BLOCK, VIRTUAL), 4.29)
    values = scale_factor * (common_weight * jnp.tile(common, (AO_BLOCKS, 1)) + own_weight * own_part)
    return values.astype(jnp.bfloat16)


def draw_live_slots(key, part):
    key_base = jax.random.fold_in(key, 11)
    key_busy = jax.random.fold_in(key, 23)
    key_chosen = jax.random.fold_in(key, 37)
    base = jax.random.randint(key_base, (DEVICE_COUNT,), 1, SLOT_DEV // 2 + 1)
    busy = jax.random.randint(key_busy, (DEVICE_COUNT,), 0, 8) == 0
    chosen = jax.random.randint(key_chosen, (), 0, DEVICE_COUNT)
    filled = jnp.logical_or(busy, jnp.arange(DEVICE_COUNT) == chosen)
    return jnp.where(filled, SLOT_DEV, base).astype(jnp.int32)


def draw_occ_index(key, part):
    middle = jax.random.permutation(jax.random.fold_in(key, 5), OCC_ALL - 2)[:OCC_BATCH - 2] + 1
    ends = jnp.array([0, OCC_ALL - 1], dtype=jnp.int32)
    values = jnp.concatenate([ends, middle.astype(jnp.int32)])
    order = jax.random.permutation(jax.random.fold_in(key, 7), OCC_BATCH)
    return jnp.take(values, order).astype(jnp.int32)


def place_ends(values, rng, least, largest):
    shape = values.shape
    place = [jax.random.randint(jax.random.fold_in(rng, axis), (), 0, shape[axis]) for axis in range(len(shape))]
    values = values.at[tuple(place)].set(least)
    longest = shape.index(max(shape))
    place[longest] = (place[longest] + 1) % shape[longest]
    return values.at[tuple(place)].set(largest)


def setup_inputs(seed: int = 0) -> dict:
    arg_keys = jax.random.split(jax.random.key(seed), 9)
    three_center = draw_three_center(jax.random.fold_in(arg_keys[8], 71), 0)
    slot_block = place_ends(jax.random.randint(arg_keys[1], (SLOT_ALL,), 0, AO_BLOCKS), jax.random.fold_in(arg_keys[1], 1), 0, AO_BLOCKS - 1).astype(jnp.int32)
    slot_aux = place_ends(jax.random.randint(arg_keys[2], (SLOT_ALL,), 0, AUX_BLOCKS_DEV), jax.random.fold_in(arg_keys[2], 1), 0, AUX_BLOCKS_DEV - 1).astype(jnp.int32)
    live_slots = draw_live_slots(jax.random.fold_in(arg_keys[8], 71), 0)
    vir_coef = draw_vir_coef(jax.random.fold_in(arg_keys[8], 71), 0)
    eps_occ = jnp.clip(jax.random.uniform(arg_keys[5], (OCC_ALL,), jnp.float32, -1.5, -0.3), -1.5, -0.3)
    eps_vir = jnp.clip(jax.random.uniform(arg_keys[6], (VIRTUAL,), jnp.float32, 0.2, 3.0), 0.2, 3.0)
    occ_index = draw_occ_index(jax.random.fold_in(arg_keys[8], 71), 0)
    return dict(three_center=three_center, slot_block=slot_block, slot_aux=slot_aux, live_slots=live_slots, vir_coef=vir_coef, eps_occ=eps_occ, eps_vir=eps_vir, occ_index=occ_index)


def reference(three_center, slot_block, slot_aux, live_slots, vir_coef, eps_occ, eps_vir, occ_index):
    coef_blocks = vir_coef.reshape(AO_BLOCKS, AO_BLOCK, VIRTUAL)

    def transform(inputs):
        blocks, block_ids, aux_ids, live_count = inputs
        coefficients = jnp.take(coef_blocks, block_ids, axis=0).astype(jnp.float32)
        products = jnp.einsum('soqn,snv->soqv', blocks.astype(jnp.float32), coefficients)
        keep = (jnp.arange(SLOT_DEV) < live_count).astype(jnp.float32)
        select = (aux_ids[:, None] == jnp.arange(AUX_BLOCKS_DEV)[None, :]).astype(jnp.float32)
        select = select * keep[:, None]
        return jnp.einsum('sk,soqv->kqov', select, products).astype(jnp.bfloat16)

    per_device = lax.map(transform, (
        three_center.reshape(DEVICE_COUNT, SLOT_DEV, OCC_BATCH, AUX_BLOCK, AO_BLOCK),
        slot_block.reshape(DEVICE_COUNT, SLOT_DEV),
        slot_aux.reshape(DEVICE_COUNT, SLOT_DEV),
        live_slots))
    half_ints = per_device.reshape(AUX_TOTAL, OCC_BATCH * VIRTUAL).astype(jnp.float32)
    coulomb = jnp.dot(half_ints.T, half_ints, preferred_element_type=jnp.float32)
    coulomb = coulomb.reshape(OCC_BATCH, VIRTUAL, OCC_BATCH, VIRTUAL)
    occ_levels = jnp.take(eps_occ, occ_index)
    denominator = (occ_levels[:, None, None, None] + occ_levels[None, None, :, None]
                   - eps_vir[None, :, None, None] - eps_vir[None, None, None, :])
    amplitudes = coulomb / denominator
    crossed = jnp.transpose(coulomb, (0, 3, 2, 1))
    pair_energy = jnp.sum(coulomb * (2.0 * coulomb - crossed) / denominator, axis=(1, 3))
    return amplitudes, pair_energy
```

```python
import functools

import jax
import jax.numpy as jnp
from jax import lax
from jax.experimental import pallas as pl
from jax.experimental.pallas import tpu as pltpu
from jax.sharding import PartitionSpec as P

AUX_BLOCKS_DEV = 2
MESH = pl.DeviceIdType.MESH
LANES = 128


def half_kernel(slots, occ, block_ref, aux_ref, live_ref, index_ref, tc_hbm, coef_hbm, eps_hbm,
                h_ref, level_ref, tc_buf, coef_buf, acc, eps_buf, tc_sem, coef_sem, eps_sem):
    span = coef_buf.shape[1]
    rows = tc_buf.shape[1] // occ
    vir = coef_buf.shape[2]
    eps_copy = pltpu.make_async_copy(eps_hbm, eps_buf, eps_sem)
    copies = []
    for s in range(slots):
        start = pl.multiple_of(block_ref[s] * span, span)
        copies.append((
            pltpu.make_async_copy(tc_hbm.at[s], tc_buf.at[s], tc_sem.at[s]),
            pltpu.make_async_copy(coef_hbm.at[pl.ds(start, span)], coef_buf.at[s], coef_sem.at[s]),
        ))
        for c in copies[-1]:
            c.start()
    eps_copy.start()
    acc[...] = jnp.zeros_like(acc)
    for s in range(slots):
        for c in copies[s]:
            c.wait()

        @pl.when(s < live_ref[0])
        def _():
            acc[aux_ref[s]] += jnp.dot(tc_buf[s], coef_buf[s], preferred_element_type=jnp.float32)

    for k in range(AUX_BLOCKS_DEV):
        for i in range(occ):
            h_ref[k * rows:(k + 1) * rows, i * vir:(i + 1) * vir] = (
                acc[k, i * rows:(i + 1) * rows, :].astype(jnp.bfloat16))
    eps_copy.wait()
    for i in range(occ):
        level_ref[i] = eps_buf[index_ref[i]]


def pair_kernel(na, nb, h_ref, level_ref, eps_ref, amp_ref, e_ref,
                held, part, core_in, out_z, in_z, turned, tiles, e_own, e_all,
                g_send, g_recv, c_send, c_recv, z_send, z_recv, t_send, t_recv, e_send, e_recv):
    me = lax.axis_index("aux")
    blk = lax.axis_index("blk")
    nz = nb // 2
    core = lax.rem(blk, 2)
    zed = lax.div(blk, 2)
    vir = eps_ref.shape[1]
    rows = vir // nb

    def aux_peer(d):
        return (lax.rem(me + d, na), blk)

    def blk_peer(d):
        return (me, lax.rem(blk + d, nb))

    def z_peer(d):
        return (me, 2 * lax.rem(zed + d, nz) + core)

    barrier = pltpu.get_barrier_semaphore()
    for d in range(1, na):
        pl.semaphore_signal(barrier, inc=1, device_id=aux_peer(d), device_id_type=MESH)
    for d in range(1, nb):
        pl.semaphore_signal(barrier, inc=1, device_id=blk_peer(d), device_id_type=MESH)
    pl.semaphore_wait(barrier, na + nb - 2)

    gathers = []
    for d in range(1, na):
        gathers.append(pltpu.make_async_remote_copy(
            src_ref=h_ref, dst_ref=held.at[d - 1], send_sem=g_send.at[d - 1], recv_sem=g_recv.at[d - 1],
            device_id=aux_peer(d), device_id_type=MESH))
        gathers[-1].start()

    own_cols = pl.ds(pl.multiple_of(me * vir, vir), vir)

    def add(src, first):
        left = jnp.transpose(src[:, own_cols])
        for j in range(na):
            cols = slice(j * vir, (j + 1) * vir)
            res = jnp.dot(left, src[:, cols], preferred_element_type=jnp.float32)
            for k in range(nb):
                piece = res[k * rows:(k + 1) * rows]
                if first:
                    part[k % 2, k // 2, :, cols] = piece
                else:
                    part[k % 2, k // 2, :, cols] += piece

    add(h_ref, True)
    for d in range(1, na):
        gathers[d - 1].wait_recv()
        add(held.at[d - 1], False)

    swap = pltpu.make_async_remote_copy(
        src_ref=part.at[1 - core], dst_ref=core_in, send_sem=c_send, recv_sem=c_recv,
        device_id=(me, 2 * zed + 1 - core), device_id_type=MESH)
    swap.start()
    swap.wait_recv()
    sends = []
    for d in range(1, nz):
        to = lax.rem(zed + d, nz)
        out_z[d - 1] = (part[core, to] + core_in[to]).astype(jnp.bfloat16)
        sends.append(pltpu.make_async_remote_copy(
            src_ref=out_z.at[d - 1], dst_ref=in_z.at[d - 1], send_sem=z_send.at[d - 1],
            recv_sem=z_recv.at[d - 1], device_id=z_peer(d), device_id_type=MESH))
        sends[-1].start()
    total = part[core, zed] + core_in[zed]
    for d in range(1, nz):
        sends[d - 1].wait_recv()
        total = total + in_z[d - 1].astype(jnp.float32)

    pieces = [total[:, j * vir:(j + 1) * vir] for j in range(na)]
    stacked = pieces
    if na * rows < LANES:
        stacked = pieces + [jnp.zeros((LANES - na * rows, vir), jnp.float32)]
    turned[...] = jnp.transpose(jnp.concatenate(stacked, axis=0))
    swaps = []
    for d in range(1, nb):
        to = lax.rem(blk + d, nb)
        swaps.append(pltpu.make_async_remote_copy(
            src_ref=turned.at[pl.ds(pl.multiple_of(to * rows, rows), rows)], dst_ref=tiles.at[blk],
            send_sem=t_send.at[d - 1], recv_sem=t_recv.at[d - 1],
            device_id=blk_peer(d), device_id_type=MESH))
        swaps[-1].start()
    tiles[blk] = turned[pl.ds(pl.multiple_of(blk * rows, rows), rows), :]

    level = eps_ref[...]
    turn = jnp.transpose(jnp.broadcast_to(level, (LANES, vir)))
    own_level = level_ref[me]
    column = jnp.zeros((rows, LANES), jnp.float32)
    for k in range(nb):
        column = jnp.where(blk == k, turn[k * rows:(k + 1) * rows], column)
    column = column[:, :1]
    ratios = []
    for j in range(na):
        ratio = pieces[j] / (((own_level + level_ref[j]) - column) - level)
        amp_ref[:, j * vir:(j + 1) * vir] = ratio
        ratios.append(ratio)

    for c in swaps:
        c.wait_recv()
    lane = lax.broadcasted_iota(jnp.int32, (rows, LANES), 1)
    lane_e = lax.broadcasted_iota(jnp.int32, (8, LANES), 1)
    per = LANES // rows
    energy = jnp.zeros((8, LANES), jnp.float32)
    for j in range(na):
        groups = []
        for g in range(vir // LANES):
            crossed = jnp.zeros((rows, LANES), jnp.float32)
            for m in range(per):
                tile = tiles[g * per + m]
                shift = (rows * (m - j)) % LANES
                if shift:
                    tile = pltpu.roll(tile, shift, 1)
                crossed = jnp.where(lax.div(lane, rows) == m, tile, crossed)
            groups.append(crossed)
        crossed = jnp.concatenate(groups, axis=1)
        value = jnp.sum(ratios[j] * (2.0 * pieces[j] - crossed))
        energy = jnp.where(lane_e == j, value, energy)
    e_own[...] = energy
    e_all[blk] = energy
    e_sends = []
    for d in range(1, nb):
        e_sends.append(pltpu.make_async_remote_copy(
            src_ref=e_own, dst_ref=e_all.at[blk], send_sem=e_send.at[d - 1], recv_sem=e_recv.at[d - 1],
            device_id=blk_peer(d), device_id_type=MESH))
        e_sends[-1].start()
    for c in e_sends:
        c.wait_recv()
    result = e_all[0]
    for k in range(1, nb):
        result = result + e_all[k]
    e_ref[...] = result[:1, :na]
    for c in gathers + [swap] + sends + swaps + e_sends:
        c.wait_send()


def body(three_center, slot_block, slot_aux, live_slots, vir_coef, eps_occ, eps_vir, occ_index):
    na = lax.axis_size("aux")
    nb = lax.axis_size("blk")
    nz = nb // 2
    slots, occ, aux_rows, span = three_center.shape
    vir = vir_coef.shape[1]
    depth = AUX_BLOCKS_DEV * aux_rows
    wide = occ * vir
    rows = vir // nb
    smem = pl.BlockSpec(memory_space=pltpu.SMEM)
    vmem = pl.BlockSpec(memory_space=pltpu.VMEM)
    anyspace = pl.BlockSpec(memory_space=pl.ANY)
    half, levels = pl.pallas_call(
        functools.partial(half_kernel, slots, occ),
        out_shape=(jax.ShapeDtypeStruct((depth, wide), jnp.bfloat16),
                   jax.ShapeDtypeStruct((occ,), jnp.float32)),
        in_specs=[smem] * 4 + [anyspace] * 3,
        out_specs=(vmem, smem),
        scratch_shapes=[
            pltpu.VMEM((slots, occ * aux_rows, span), jnp.bfloat16),
            pltpu.VMEM((slots, span, vir), jnp.bfloat16),
            pltpu.VMEM((AUX_BLOCKS_DEV, occ * aux_rows, vir), jnp.float32),
            pltpu.SMEM((eps_occ.shape[0],), jnp.float32),
            pltpu.SemaphoreType.DMA((slots,)),
            pltpu.SemaphoreType.DMA((slots,)),
            pltpu.SemaphoreType.DMA,
        ],
    )(slot_block, slot_aux, live_slots, occ_index,
      three_center.reshape(slots, occ * aux_rows, span), vir_coef, eps_occ)
    dma = pltpu.SemaphoreType.DMA
    amp, energy = pl.pallas_call(
        functools.partial(pair_kernel, na, nb),
        out_shape=(jax.ShapeDtypeStruct((rows, wide), jnp.float32),
                   jax.ShapeDtypeStruct((1, na), jnp.float32)),
        in_specs=[vmem, smem, vmem],
        out_specs=(vmem, vmem),
        scratch_shapes=[
            pltpu.VMEM((na - 1, depth, wide), jnp.bfloat16),
            pltpu.VMEM((2, nz, rows, wide), jnp.float32),
            pltpu.VMEM((nz, rows, wide), jnp.float32),
            pltpu.VMEM((nz - 1, rows, wide), jnp.bfloat16),
            pltpu.VMEM((nz - 1, rows, wide), jnp.bfloat16),
            pltpu.VMEM((vir, LANES), jnp.float32),
            pltpu.VMEM((nb, rows, LANES), jnp.float32),
            pltpu.VMEM((8, LANES), jnp.float32),
            pltpu.VMEM((nb, 8, LANES), jnp.float32),
            dma((na - 1,)), dma((na - 1,)), dma, dma, dma((nz - 1,)), dma((nz - 1,)),
            dma((nb - 1,)), dma((nb - 1,)), dma((nb - 1,)), dma((nb - 1,)),
        ],
        compiler_params=pltpu.CompilerParams(collective_id=0, has_side_effects=True),
    )(half, levels, eps_vir.reshape(1, vir))
    return amp.reshape(1, rows, occ, vir), energy


def solution(mesh):
    in_specs = (
        P(("aux", "blk"), None, None, None),
        P(("aux", "blk")),
        P(("aux", "blk")),
        P(("aux", "blk")),
        P(),
        P(),
        P(),
        P(),
    )
    out_specs = (P("aux", "blk", None, None), P("aux", None))
    return jax.shard_map(body, mesh=mesh, in_specs=in_specs, out_specs=out_specs, check_vma=False)
```

```python
import functools

import jax
import jax.numpy as jnp
from jax import lax
from jax.experimental import pallas as pl
from jax.experimental.pallas import tpu as pltpu
from jax.sharding import PartitionSpec as P

AUX_BLOCKS_DEV = 2
MESH = pl.DeviceIdType.MESH
LANES = 128


def pair_kernel(na, nb, slots, block_ref, aux_ref, live_ref, index_ref, tc_hbm, coef_hbm, eps_hbm, eps_ref,
                amp_ref, e_ref,
                tc_buf, coef_buf, weights, eps_buf, half, held, part, core_in, out_z, in_z, turned, tiles,
                e_own, e_all, tc_sem, coef_sem, eps_sem,
                g_send, g_recv, c_send, c_recv, z_send, z_recv, t_send, t_recv, e_send, e_recv):
    me = lax.axis_index("aux")
    blk = lax.axis_index("blk")
    nz = nb // 2
    core = lax.rem(blk, 2)
    zed = lax.div(blk, 2)
    vir = eps_ref.shape[1]
    rows = vir // nb
    span = tc_buf.shape[3]
    depth = tc_buf.shape[2]
    ring = na == 4

    def blk_peer(d):
        return (me, lax.rem(blk + d, nb))

    def z_peer(d):
        return (me, 2 * lax.rem(zed + d, nz) + core)

    if ring:
        after = (lax.rem(me, 2) * 2 + 1 - lax.div(me, 2), blk)
        before = ((1 - lax.rem(me, 2)) * 2 + lax.div(me, 2), blk)
        aux_peers = [after, before]
    else:
        aux_peers = [(lax.rem(me + d, na), blk) for d in range(1, na)]
    barrier = pltpu.get_barrier_semaphore()
    for peer in aux_peers + [blk_peer(d) for d in range(1, nb)]:
        pl.semaphore_signal(barrier, inc=1, device_id=peer, device_id_type=MESH)

    loads = []
    chunks = coef_sem.shape[0]
    per_chunk = coef_buf.shape[0] // chunks
    for n in range(chunks):
        part_of = pl.ds(n * per_chunk, per_chunk)
        loads.append(pltpu.make_async_copy(coef_hbm.at[part_of], coef_buf.at[part_of], coef_sem.at[n]))
    tc_loads = [pltpu.make_async_copy(tc_hbm.at[s], tc_buf.at[s], tc_sem.at[s]) for s in range(slots)]
    eps_load = pltpu.make_async_copy(eps_hbm, eps_buf, eps_sem)
    for c in loads + tc_loads + [eps_load]:
        c.start()
    for c in loads:
        c.wait()
    for s in range(slots):
        block = coef_buf[block_ref[s]]
        for k in range(AUX_BLOCKS_DEV):
            used = jnp.logical_and(s < live_ref[0], aux_ref[s] == k)
            scale = jnp.where(used, 1.0, 0.0).astype(jnp.float32)
            weights[s * span:(s + 1) * span, k * vir:(k + 1) * vir] = (
                block.astype(jnp.float32) * scale).astype(jnp.bfloat16)
    for c in tc_loads:
        c.wait()

    def transform(i):
        left = jnp.concatenate([tc_buf[s, i] for s in range(slots)], axis=1)
        res = jnp.dot(left, weights[...], preferred_element_type=jnp.float32)
        for k in range(AUX_BLOCKS_DEV):
            half[i, k * depth:(k + 1) * depth, :] = res[:, k * vir:(k + 1) * vir].astype(jnp.bfloat16)

    def remote(src, slot, j, peer):
        return pltpu.make_async_remote_copy(
            src_ref=src, dst_ref=held.at[slot, j], send_sem=g_send.at[slot, j], recv_sem=g_recv.at[slot, j],
            device_id=peer, device_id_type=MESH)

    def add(src, first):
        left = jnp.transpose(src[me])
        for j in range(na):
            cols = slice(j * vir, (j + 1) * vir)
            res = jnp.dot(left, src[j], preferred_element_type=jnp.float32)
            for k in range(nb):
                piece = res[k * rows:(k + 1) * rows]
                if first:
                    part[k % 2, k // 2, :, cols] = piece
                else:
                    part[k % 2, k // 2, :, cols] += piece

    gathers = []
    if ring:
        to_after = [remote(half.at[j], 0, j, after) for j in range(na)]
        to_before = [remote(half.at[j], 2, j, before) for j in range(na)]
        transform(0)
        pl.semaphore_wait(barrier, len(aux_peers) + nb - 1)
        to_after[0].start()
        transform(2)
        to_before[2].start()
        transform(1)
        to_after[1].start()
        transform(3)
        to_before[3].start()
        for j in (2, 3):
            to_after[j].start()
        for j in (0, 1):
            to_before[j].start()
        passed = [remote(held.at[0, j], 1, j, after) for j in (0, 1)]
        passed += [remote(held.at[2, j], 1, j, before) for j in (2, 3)]
        for early, late in ((0, 2), (1, 3)):
            to_after[early].wait_recv()
            passed[early].start()
            to_before[late].wait_recv()
            passed[late].start()
        add(half, True)
        for j in (2, 3):
            to_after[j].wait_recv()
        add(held.at[0], False)
        for j in (0, 1):
            to_before[j].wait_recv()
        add(held.at[2], False)
        for c in passed:
            c.wait_recv()
        add(held.at[1], False)
        gathers = to_after + to_before + passed
    else:
        for j in range(na):
            transform(j)
        pl.semaphore_wait(barrier, len(aux_peers) + nb - 1)
        for d in range(1, na):
            for j in range(na):
                gathers.append(remote(half.at[j], d - 1, j, aux_peers[d - 1]))
                gathers[-1].start()
        add(half, True)
        for d in range(1, na):
            for j in range(na):
                gathers[(d - 1) * na + j].wait_recv()
            add(held.at[d - 1], False)
    eps_load.wait()

    swap = pltpu.make_async_remote_copy(
        src_ref=part.at[1 - core], dst_ref=core_in, send_sem=c_send, recv_sem=c_recv,
        device_id=(me, 2 * zed + 1 - core), device_id_type=MESH)
    swap.start()
    swap.wait_recv()
    sends = []
    for d in range(1, nz):
        to = lax.rem(zed + d, nz)
        out_z[d - 1] = (part[core, to] + core_in[to]).astype(jnp.bfloat16)
        sends.append(pltpu.make_async_remote_copy(
            src_ref=out_z.at[d - 1], dst_ref=in_z.at[d - 1], send_sem=z_send.at[d - 1],
            recv_sem=z_recv.at[d - 1], device_id=z_peer(d), device_id_type=MESH))
        sends[-1].start()
    total = part[core, zed] + core_in[zed]
    for d in range(1, nz):
        sends[d - 1].wait_recv()
        total = total + in_z[d - 1].astype(jnp.float32)

    pieces = [total[:, j * vir:(j + 1) * vir] for j in range(na)]
    stacked = pieces
    if na * rows < LANES:
        stacked = pieces + [jnp.zeros((LANES - na * rows, vir), jnp.float32)]
    turned[...] = jnp.transpose(jnp.concatenate(stacked, axis=0))
    swaps = []
    for d in range(1, nb):
        to = lax.rem(blk + d, nb)
        swaps.append(pltpu.make_async_remote_copy(
            src_ref=turned.at[pl.ds(pl.multiple_of(to * rows, rows), rows)], dst_ref=tiles.at[blk],
            send_sem=t_send.at[d - 1], recv_sem=t_recv.at[d - 1],
            device_id=blk_peer(d), device_id_type=MESH))
        swaps[-1].start()
    tiles[blk] = turned[pl.ds(pl.multiple_of(blk * rows, rows), rows), :]

    level = eps_ref[...]
    turn = jnp.transpose(jnp.broadcast_to(level, (LANES, vir)))
    own_level = eps_buf[index_ref[me]]
    column = jnp.zeros((rows, LANES), jnp.float32)
    for k in range(nb):
        column = jnp.where(blk == k, turn[k * rows:(k + 1) * rows], column)
    column = column[:, :1]
    ratios = []
    for j in range(na):
        ratio = pieces[j] / (((own_level + eps_buf[index_ref[j]]) - column) - level)
        amp_ref[0, :, j, :] = ratio
        ratios.append(ratio)

    for c in swaps:
        c.wait_recv()
    lane = lax.broadcasted_iota(jnp.int32, (rows, LANES), 1)
    lane_e = lax.broadcasted_iota(jnp.int32, (8, LANES), 1)
    per = LANES // rows
    energy = jnp.zeros((8, LANES), jnp.float32)
    for j in range(na):
        groups = []
        for g in range(vir // LANES):
            crossed = jnp.zeros((rows, LANES), jnp.float32)
            for m in range(per):
                tile = tiles[g * per + m]
                shift = (rows * (m - j)) % LANES
                if shift:
                    tile = pltpu.roll(tile, shift, 1)
                crossed = jnp.where(lax.div(lane, rows) == m, tile, crossed)
            groups.append(crossed)
        crossed = jnp.concatenate(groups, axis=1)
        value = jnp.sum(ratios[j] * (2.0 * pieces[j] - crossed))
        energy = jnp.where(lane_e == j, value, energy)
    e_own[...] = energy
    e_all[blk] = energy
    e_sends = []
    for d in range(1, nb):
        e_sends.append(pltpu.make_async_remote_copy(
            src_ref=e_own, dst_ref=e_all.at[blk], send_sem=e_send.at[d - 1], recv_sem=e_recv.at[d - 1],
            device_id=blk_peer(d), device_id_type=MESH))
        e_sends[-1].start()
    for c in e_sends:
        c.wait_recv()
    result = e_all[0]
    for k in range(1, nb):
        result = result + e_all[k]
    e_ref[...] = result[:1, :na]
    for c in gathers + [swap] + sends + swaps + e_sends:
        c.wait_send()


def body(three_center, slot_block, slot_aux, live_slots, vir_coef, eps_occ, eps_vir, occ_index):
    na = lax.axis_size("aux")
    nb = lax.axis_size("blk")
    nz = nb // 2
    slots, occ, aux_rows, span = three_center.shape
    vir = vir_coef.shape[1]
    depth = AUX_BLOCKS_DEV * aux_rows
    wide = occ * vir
    rows = vir // nb
    smem = pl.BlockSpec(memory_space=pltpu.SMEM)
    vmem = pl.BlockSpec(memory_space=pltpu.VMEM)
    anyspace = pl.BlockSpec(memory_space=pl.ANY)
    blocks = vir_coef.shape[0] // span
    chunks = max(n for n in range(1, 9) if blocks % n == 0)
    dma = pltpu.SemaphoreType.DMA
    return pl.pallas_call(
        functools.partial(pair_kernel, na, nb, slots),
        out_shape=(jax.ShapeDtypeStruct((1, rows, occ, vir), jnp.float32),
                   jax.ShapeDtypeStruct((1, na), jnp.float32)),
        in_specs=[smem] * 4 + [anyspace] * 3 + [vmem],
        out_specs=(vmem, vmem),
        scratch_shapes=[
            pltpu.VMEM((slots, occ, aux_rows, span), jnp.bfloat16),
            pltpu.VMEM((blocks, span, vir), jnp.bfloat16),
            pltpu.VMEM((slots * span, AUX_BLOCKS_DEV * vir), jnp.bfloat16),
            pltpu.SMEM((eps_occ.shape[0],), jnp.float32),
            pltpu.VMEM((occ, depth, vir), jnp.bfloat16),
            pltpu.VMEM((na - 1, occ, depth, vir), jnp.bfloat16),
            pltpu.VMEM((2, nz, rows, wide), jnp.float32),
            pltpu.VMEM((nz, rows, wide), jnp.float32),
            pltpu.VMEM((nz - 1, rows, wide), jnp.bfloat16),
            pltpu.VMEM((nz - 1, rows, wide), jnp.bfloat16),
            pltpu.VMEM((vir, LANES), jnp.float32),
            pltpu.VMEM((nb, rows, LANES), jnp.float32),
            pltpu.VMEM((8, LANES), jnp.float32),
            pltpu.VMEM((nb, 8, LANES), jnp.float32),
            dma((slots,)), dma((chunks,)), dma,
            dma((na - 1, na)), dma((na - 1, na)), dma, dma, dma((nz - 1,)), dma((nz - 1,)),
            dma((nb - 1,)), dma((nb - 1,)), dma((nb - 1,)), dma((nb - 1,)),
        ],
        compiler_params=pltpu.CompilerParams(collective_id=0, has_side_effects=True),
    )(slot_block, slot_aux, live_slots, occ_index, three_center,
      vir_coef.reshape(blocks, span, vir), eps_occ, eps_vir.reshape(1, vir))


def solution(mesh):
    in_specs = (
        P(("aux", "blk"), None, None, None),
        P(("aux", "blk")),
        P(("aux", "blk")),
        P(("aux", "blk")),
        P(),
        P(),
        P(),
        P(),
    )
    out_specs = (P("aux", "blk", None, None), P("aux", None))
    return jax.shard_map(body, mesh=mesh, in_specs=in_specs, out_specs=out_specs, check_vma=False)
```

```python
import functools

import jax
import jax.numpy as jnp
from jax import lax
from jax.experimental import pallas as pl
from jax.experimental.pallas import tpu as pltpu
from jax.sharding import PartitionSpec as P

AUX_BLOCKS_DEV = 2
MESH = pl.DeviceIdType.MESH
LANES = 128


def pair_kernel(na, nb, slots, block_ref, aux_ref, live_ref, index_ref, tc_hbm, coef_hbm, eps_hbm, eps_ref,
                amp_ref, e_ref,
                tc_buf, coef_buf, weights, eps_buf, half, held, part, core_in, out_z, in_z, turned, tiles,
                packs, tail, e_own, e_all, e_tail, tc_sem, coef_sem, eps_sem,
                g_send, g_recv, c_send, c_recv, z_send, z_recv, t_send, t_recv, n_send, n_recv,
                e_send, e_recv, f_send, f_recv):
    me = lax.axis_index("aux")
    blk = lax.axis_index("blk")
    nz = nb // 2
    core = lax.rem(blk, 2)
    zed = lax.div(blk, 2)
    vir = eps_ref.shape[1]
    rows = vir // nb
    span = tc_buf.shape[3]
    depth = tc_buf.shape[2]
    ring = na == 4
    kept = na // 2 + 1
    rest = na - kept

    def gray(x):
        return lax.div(x, 2) * 2 + lax.rem(lax.rem(x, 2) + lax.div(x, 2), 2)

    def at(t):
        if ring:
            return gray(lax.rem(gray(me) + t % na, na))
        return lax.rem(me + t % na, na)

    def blk_peer(d):
        return (me, lax.rem(blk + d, nb))

    def z_peer(d):
        return (me, 2 * lax.rem(zed + d, nz) + core)

    steps = (1, na - 1) if ring else tuple(range(1, na))
    barrier = pltpu.get_barrier_semaphore()
    sources = [(at(-d), blk) for d in steps] + [blk_peer(d) for d in range(1, nb)]
    for u in range(1, rest + 1):
        sources += [(at(-u), lax.rem(blk + d, nb)) for d in range(1, nb)]
    for peer in sources:
        pl.semaphore_signal(barrier, inc=1, device_id=peer, device_id_type=MESH)

    loads = []
    chunks = coef_sem.shape[0]
    per_chunk = coef_buf.shape[0] // chunks
    for n in range(chunks):
        part_of = pl.ds(n * per_chunk, per_chunk)
        loads.append(pltpu.make_async_copy(coef_hbm.at[part_of], coef_buf.at[part_of], coef_sem.at[n]))
    tc_loads = [pltpu.make_async_copy(tc_hbm.at[s], tc_buf.at[s], tc_sem.at[s]) for s in range(slots)]
    eps_load = pltpu.make_async_copy(eps_hbm, eps_buf, eps_sem)
    for c in loads + tc_loads + [eps_load]:
        c.start()
    for c in loads:
        c.wait()
    for s in range(slots):
        block = coef_buf[block_ref[s]]
        for k in range(AUX_BLOCKS_DEV):
            used = jnp.logical_and(s < live_ref[0], aux_ref[s] == k)
            scale = jnp.where(used, 1.0, 0.0).astype(jnp.float32)
            weights[s * span:(s + 1) * span, k * vir:(k + 1) * vir] = (
                block.astype(jnp.float32) * scale).astype(jnp.bfloat16)
    for c in tc_loads:
        c.wait()

    def transform(i):
        left = jnp.concatenate([tc_buf[s, i] for s in range(slots)], axis=1)
        res = jnp.dot(left, weights[...], preferred_element_type=jnp.float32)
        for k in range(AUX_BLOCKS_DEV):
            half[i, k * depth:(k + 1) * depth, :] = res[:, k * vir:(k + 1) * vir].astype(jnp.bfloat16)

    def remote(src, dst, slot, n, peer):
        return pltpu.make_async_remote_copy(
            src_ref=src, dst_ref=dst, send_sem=g_send.at[slot, n], recv_sem=g_recv.at[slot, n],
            device_id=peer, device_id_type=MESH)

    def add(block, first):
        left = jnp.transpose(block(0))
        for t in range(kept):
            cols = slice(t * vir, (t + 1) * vir)
            res = jnp.dot(left, block(t), preferred_element_type=jnp.float32)
            for k in range(nb):
                piece = res[k * rows:(k + 1) * rows]
                if first:
                    part[k % 2, k // 2, :, cols] = piece
                else:
                    part[k % 2, k // 2, :, cols] += piece

    for i in range(na):
        transform(i)
    pl.semaphore_wait(barrier, len(sources))
    if ring:
        after, before = (at(1), blk), (at(-1), blk)
        mid = AUX_BLOCKS_DEV * depth // 2
        low, high = pl.ds(0, mid), pl.ds(mid, mid)
        to_after = [remote(half.at[at(1 + t)], held.at[0, t], 0, t, after) for t in range(kept)]
        to_before = [remote(half.at[at(t - 1)], held.at[2, t], 2, t, before) for t in range(kept)]
        for c in (to_after[1], to_before[1], to_after[2], to_before[0], to_after[0], to_before[2]):
            c.start()
        passed = [
            remote(held.at[0, 1], held.at[1, 0], 1, 0, after),
            remote(held.at[0, 2, low], held.at[1, 1, low], 1, 1, after),
            remote(held.at[2, 1], held.at[1, 2], 1, 2, before),
            remote(held.at[2, 0, high], held.at[1, 1, high], 1, 3, before),
        ]
        for got, on in ((to_after[1], 0), (to_before[1], 2), (to_after[2], 1), (to_before[0], 3)):
            got.wait_recv()
            passed[on].start()
        add(lambda t: half[at(t)], True)
        to_after[0].wait_recv()
        add(lambda t: held[0, t], False)
        to_before[2].wait_recv()
        add(lambda t: held[2, t], False)
        for c in passed:
            c.wait_recv()
        add(lambda t: held[1, t], False)
        gathers = to_after + to_before + passed
    else:
        gathers = []
        for d in range(1, na):
            for t in range(kept):
                gathers.append(remote(half.at[at(d + t)], held.at[d - 1, t], d - 1, t, (at(d), blk)))
                gathers[-1].start()
        add(lambda t: half[at(t)], True)
        for d in range(1, na):
            for t in range(kept):
                gathers[(d - 1) * kept + t].wait_recv()
            add(lambda t: held[d - 1, t], False)
    eps_load.wait()

    swap = pltpu.make_async_remote_copy(
        src_ref=part.at[1 - core], dst_ref=core_in, send_sem=c_send, recv_sem=c_recv,
        device_id=(me, 2 * zed + 1 - core), device_id_type=MESH)
    swap.start()
    swap.wait_recv()
    sends = []
    for d in range(1, nz):
        to = lax.rem(zed + d, nz)
        out_z[d - 1] = (part[core, to] + core_in[to]).astype(jnp.bfloat16)
        sends.append(pltpu.make_async_remote_copy(
            src_ref=out_z.at[d - 1], dst_ref=in_z.at[d - 1], send_sem=z_send.at[d - 1],
            recv_sem=z_recv.at[d - 1], device_id=z_peer(d), device_id_type=MESH))
        sends[-1].start()
    total = part[core, zed] + core_in[zed]
    for d in range(1, nz):
        sends[d - 1].wait_recv()
        total = total + in_z[d - 1].astype(jnp.float32)

    pieces = [total[:, t * vir:(t + 1) * vir] for t in range(kept)]
    stacked = pieces
    if kept * rows < LANES:
        stacked = pieces + [jnp.zeros((LANES - kept * rows, vir), jnp.float32)]
    flat = jnp.transpose(jnp.concatenate(stacked, axis=0))
    turned[...] = flat
    lane = lax.broadcasted_iota(jnp.int32, (rows, LANES), 1)
    lane_e = lax.broadcasted_iota(jnp.int32, (8, LANES), 1)
    per = LANES // rows
    bands = rows // 8

    def rolled(value, shift):
        shift = shift % LANES
        return pltpu.roll(value, shift, 1) if shift else value

    for u in range(1, rest + 1):
        for k in range(nb):
            packed = jnp.zeros((8, LANES), jnp.float32)
            for q in range(bands):
                band = flat[k * rows + 8 * q:k * rows + 8 * q + 8]
                packed = jnp.where(lax.div(lane_e, rows) == q, rolled(band, rows * (q - u)), packed)
            packs[u - 1, k] = packed
    tails = []
    for u in range(1, rest + 1):
        for d in range(nb):
            to = lax.rem(blk + d, nb)
            tails.append(pltpu.make_async_remote_copy(
                src_ref=packs.at[u - 1, to], dst_ref=tail.at[u - 1, blk],
                send_sem=n_send.at[u - 1, d], recv_sem=n_recv.at[u - 1, d],
                device_id=(at(u), to), device_id_type=MESH))
            tails[-1].start()
    swaps = []
    for d in range(1, nb):
        to = lax.rem(blk + d, nb)
        swaps.append(pltpu.make_async_remote_copy(
            src_ref=turned.at[pl.ds(pl.multiple_of(to * rows, rows), rows)], dst_ref=tiles.at[blk],
            send_sem=t_send.at[d - 1], recv_sem=t_recv.at[d - 1],
            device_id=blk_peer(d), device_id_type=MESH))
        swaps[-1].start()
    tiles[blk] = turned[pl.ds(pl.multiple_of(blk * rows, rows), rows), :]

    level = eps_ref[...]
    turn = jnp.transpose(jnp.broadcast_to(level, (LANES, vir)))
    own_level = eps_buf[index_ref[me]]
    column = jnp.zeros((rows, LANES), jnp.float32)
    for k in range(nb):
        column = jnp.where(blk == k, turn[k * rows:(k + 1) * rows], column)
    column = column[:, :1]
    def ratio_of(t, piece):
        return piece / (((own_level + eps_buf[index_ref[at(t)]]) - column) - level)

    ratios = [ratio_of(t, pieces[t]) for t in range(kept)]
    scores = [ratios[t] * pieces[t] * 2.0 for t in range(kept)]
    for c in swaps:
        c.wait_recv()
    energy = jnp.zeros((8, LANES), jnp.float32)
    for t in range(kept):
        groups = []
        for g in range(vir // LANES):
            crossed = jnp.zeros((rows, LANES), jnp.float32)
            for m in range(per):
                crossed = jnp.where(lax.div(lane, rows) == m, rolled(tiles[g * per + m], rows * (m - t)), crossed)
            groups.append(crossed)
        crossed = jnp.concatenate(groups, axis=1)
        value = jnp.sum(scores[t] - ratios[t] * crossed)
        energy = jnp.where(lane_e == t, value, energy)
    e_own[...] = energy
    e_all[blk] = energy
    e_sends = []
    for d in range(1, nb):
        e_sends.append(pltpu.make_async_remote_copy(
            src_ref=e_own, dst_ref=e_all.at[blk], send_sem=e_send.at[d - 1], recv_sem=e_recv.at[d - 1],
            device_id=blk_peer(d), device_id_type=MESH))
        e_sends[-1].start()
    for u in range(1, rest + 1):
        for d in range(nb):
            e_sends.append(pltpu.make_async_remote_copy(
                src_ref=e_own, dst_ref=e_tail.at[u - 1, blk],
                send_sem=f_send.at[u - 1, d], recv_sem=f_recv.at[u - 1, d],
                device_id=(at(u), lax.rem(blk + d, nb)), device_id_type=MESH))
            e_sends[-1].start()

    for c in tails:
        c.wait_recv()
    for u in range(rest, 0, -1):
        groups = []
        for g in range(vir // LANES):
            strips = []
            for q in range(bands):
                strip = jnp.zeros((8, LANES), jnp.float32)
                for m in range(per):
                    moved = rolled(tail[u - 1, g * per + m], rows * (m - q))
                    strip = jnp.where(lax.div(lane_e, rows) == m, moved, strip)
                strips.append(strip)
            groups.append(jnp.concatenate(strips, axis=0))
        ratios.append(ratio_of(na - u, jnp.concatenate(groups, axis=1)))
    for j in range(na):
        chosen = ratios[0]
        for t in range(1, na):
            chosen = jnp.where(at(t) == j, ratios[t], chosen)
        amp_ref[0, :, j, :] = chosen

    for c in e_sends:
        c.wait_recv()
    sums = [e_all[...]] + [e_tail[u - 1] for u in range(1, rest + 1)]
    totals = []
    for group in sums:
        result = group[0]
        for k in range(1, nb):
            result = result + group[k]
        totals.append(result)
    final = jnp.zeros((8, LANES), jnp.float32)
    for t in range(na):
        group, place = (totals[0], t) if t < kept else (totals[na - t], na - t)
        value = jnp.sum(jnp.where(lane_e == place, group, 0.0)[:1], axis=1, keepdims=True)
        final = jnp.where(lane_e == at(t), value, final)
    e_ref[...] = final[:1, :na]
    for c in gathers + [swap] + sends + swaps + tails + e_sends:
        c.wait_send()


def body(three_center, slot_block, slot_aux, live_slots, vir_coef, eps_occ, eps_vir, occ_index):
    na = lax.axis_size("aux")
    nb = lax.axis_size("blk")
    nz = nb // 2
    slots, occ, aux_rows, span = three_center.shape
    vir = vir_coef.shape[1]
    depth = AUX_BLOCKS_DEV * aux_rows
    kept = na // 2 + 1
    rest = na - kept
    wide = kept * vir
    rows = vir // nb
    smem = pl.BlockSpec(memory_space=pltpu.SMEM)
    vmem = pl.BlockSpec(memory_space=pltpu.VMEM)
    anyspace = pl.BlockSpec(memory_space=pl.ANY)
    blocks = vir_coef.shape[0] // span
    chunks = max(n for n in range(1, 9) if blocks % n == 0)
    dma = pltpu.SemaphoreType.DMA
    return pl.pallas_call(
        functools.partial(pair_kernel, na, nb, slots),
        out_shape=(jax.ShapeDtypeStruct((1, rows, occ, vir), jnp.float32),
                   jax.ShapeDtypeStruct((1, na), jnp.float32)),
        in_specs=[smem] * 4 + [anyspace] * 3 + [vmem],
        out_specs=(vmem, vmem),
        scratch_shapes=[
            pltpu.VMEM((slots, occ, aux_rows, span), jnp.bfloat16),
            pltpu.VMEM((blocks, span, vir), jnp.bfloat16),
            pltpu.VMEM((slots * span, AUX_BLOCKS_DEV * vir), jnp.bfloat16),
            pltpu.SMEM((eps_occ.shape[0],), jnp.float32),
            pltpu.VMEM((occ, depth, vir), jnp.bfloat16),
            pltpu.VMEM((na - 1, kept, depth, vir), jnp.bfloat16),
            pltpu.VMEM((2, nz, rows, wide), jnp.float32),
            pltpu.VMEM((nz, rows, wide), jnp.float32),
            pltpu.VMEM((nz - 1, rows, wide), jnp.bfloat16),
            pltpu.VMEM((nz - 1, rows, wide), jnp.bfloat16),
            pltpu.VMEM((vir, LANES), jnp.float32),
            pltpu.VMEM((nb, rows, LANES), jnp.float32),
            pltpu.VMEM((rest, nb, 8, LANES), jnp.float32),
            pltpu.VMEM((rest, nb, 8, LANES), jnp.float32),
            pltpu.VMEM((8, LANES), jnp.float32),
            pltpu.VMEM((nb, 8, LANES), jnp.float32),
            pltpu.VMEM((rest, nb, 8, LANES), jnp.float32),
            dma((slots,)), dma((chunks,)), dma,
            dma((na - 1, kept + 1)), dma((na - 1, kept + 1)), dma, dma, dma((nz - 1,)), dma((nz - 1,)),
            dma((nb - 1,)), dma((nb - 1,)), dma((rest, nb)), dma((rest, nb)),
            dma((nb - 1,)), dma((nb - 1,)), dma((rest, nb)), dma((rest, nb)),
        ],
        compiler_params=pltpu.CompilerParams(collective_id=0, has_side_effects=True),
    )(slot_block, slot_aux, live_slots, occ_index, three_center,
      vir_coef.reshape(blocks, span, vir), eps_occ, eps_vir.reshape(1, vir))


def solution(mesh):
    in_specs = (
        P(("aux", "blk"), None, None, None),
        P(("aux", "blk")),
        P(("aux", "blk")),
        P(("aux", "blk")),
        P(),
        P(),
        P(),
        P(),
    )
    out_specs = (P("aux", "blk", None, None), P("aux", None))
    return jax.shard_map(body, mesh=mesh, in_specs=in_specs, out_specs=out_specs, check_vma=False)
```

```python
import functools

import jax
import jax.numpy as jnp
from jax import lax
from jax.experimental import pallas as pl
from jax.experimental.pallas import tpu as pltpu
from jax.sharding import PartitionSpec as P

AUX_BLOCKS_DEV = 2
MESH = pl.DeviceIdType.MESH
LANES = 128


def pair_kernel(na, nb, slots, block_ref, aux_ref, live_ref, index_ref, tc_hbm, coef_hbm, eps_hbm, eps_ref,
                amp_ref, e_ref,
                tc_buf, coef_buf, weights, eps_buf, half, held, part, core_in, out_z, in_z, turned, tiles,
                packs, tail, e_own, e_all, e_tail, tc_sem, coef_sem, eps_sem,
                g_send, g_recv, c_send, c_recv, z_send, z_recv, t_send, t_recv, n_send, n_recv,
                e_send, e_recv, f_send, f_recv):
    me = lax.axis_index("aux")
    blk = lax.axis_index("blk")
    nz = nb // 2
    core = lax.rem(blk, 2)
    zed = lax.div(blk, 2)
    vir = eps_ref.shape[1]
    rows = vir // nb
    span = tc_buf.shape[3]
    depth = tc_buf.shape[2]
    ring = na == 4
    kept = na // 2 + 1
    rest = na - kept

    def gray(x):
        return lax.div(x, 2) * 2 + lax.rem(lax.rem(x, 2) + lax.div(x, 2), 2)

    def at(t):
        if ring:
            return gray(lax.rem(gray(me) + t % na, na))
        return lax.rem(me + t % na, na)

    def blk_peer(d):
        return (me, lax.rem(blk + d, nb))

    def z_peer(d):
        return (me, 2 * lax.rem(zed + d, nz) + core)

    steps = (1, na - 1) if ring else tuple(range(1, na))
    barrier = pltpu.get_barrier_semaphore()
    sources = [(at(-d), blk) for d in steps] + [blk_peer(d) for d in range(1, nb)]
    for u in range(1, rest + 1):
        sources += [(at(-u), lax.rem(blk + d, nb)) for d in range(1, nb)]
    for peer in sources:
        pl.semaphore_signal(barrier, inc=1, device_id=peer, device_id_type=MESH)

    loads = []
    chunks = coef_sem.shape[0]
    per_chunk = coef_buf.shape[0] // chunks
    for n in range(chunks):
        part_of = pl.ds(n * per_chunk, per_chunk)
        loads.append(pltpu.make_async_copy(coef_hbm.at[part_of], coef_buf.at[part_of], coef_sem.at[n]))
    tc_loads = [pltpu.make_async_copy(tc_hbm.at[s], tc_buf.at[s], tc_sem.at[s]) for s in range(slots)]
    eps_load = pltpu.make_async_copy(eps_hbm, eps_buf, eps_sem)
    for c in loads + tc_loads + [eps_load]:
        c.start()
    for c in loads:
        c.wait()
    for s in range(slots):
        block = coef_buf[block_ref[s]]
        for k in range(AUX_BLOCKS_DEV):
            used = jnp.logical_and(s < live_ref[0], aux_ref[s] == k)
            scale = jnp.where(used, 1.0, 0.0).astype(jnp.float32)
            weights[s * span:(s + 1) * span, k * vir:(k + 1) * vir] = (
                block.astype(jnp.float32) * scale).astype(jnp.bfloat16)
    for c in tc_loads:
        c.wait()

    def transform(i):
        left = jnp.concatenate([tc_buf[s, i] for s in range(slots)], axis=1)
        res = jnp.dot(left, weights[...], preferred_element_type=jnp.float32)
        for k in range(AUX_BLOCKS_DEV):
            half[i, k * depth:(k + 1) * depth, :] = res[:, k * vir:(k + 1) * vir].astype(jnp.bfloat16)

    def remote(src, dst, slot, n, peer):
        return pltpu.make_async_remote_copy(
            src_ref=src, dst_ref=dst, send_sem=g_send.at[slot, n], recv_sem=g_recv.at[slot, n],
            device_id=peer, device_id_type=MESH)

    def add(block, first):
        left = jnp.transpose(block(0))
        for t in range(kept):
            cols = slice(t * vir, (t + 1) * vir)
            res = jnp.dot(left, block(t), preferred_element_type=jnp.float32)
            for k in range(nb):
                piece = res[k * rows:(k + 1) * rows]
                if first:
                    part[k % 2, k // 2, :, cols] = piece
                else:
                    part[k % 2, k // 2, :, cols] += piece

    for i in range(na):
        transform(i)
    pl.semaphore_wait(barrier, len(sources))
    if ring:
        after, before = (at(1), blk), (at(-1), blk)
        mid = AUX_BLOCKS_DEV * depth // 2
        low, high = pl.ds(0, mid), pl.ds(mid, mid)
        to_after = [remote(half.at[at(1 + t)], held.at[0, t], 0, t, after) for t in range(kept)]
        to_before = [remote(half.at[at(t - 1)], held.at[2, t], 2, t, before) for t in range(kept)]
        for c in (to_after[1], to_before[1], to_after[2], to_before[0], to_after[0], to_before[2]):
            c.start()
        passed = [
            remote(held.at[0, 1], held.at[1, 0], 1, 0, after),
            remote(held.at[0, 2, low], held.at[1, 1, low], 1, 1, after),
            remote(held.at[2, 1], held.at[1, 2], 1, 2, before),
            remote(held.at[2, 0, high], held.at[1, 1, high], 1, 3, before),
        ]
        for got, on in ((to_after[1], 0), (to_before[1], 2), (to_after[2], 1), (to_before[0], 3)):
            got.wait_recv()
            passed[on].start()
        add(lambda t: half[at(t)], True)
        to_after[0].wait_recv()
        add(lambda t: held[0, t], False)
        to_before[2].wait_recv()
        add(lambda t: held[2, t], False)
        for c in passed:
            c.wait_recv()
        add(lambda t: held[1, t], False)
        gathers = to_after + to_before + passed
    else:
        gathers = []
        for d in range(1, na):
            for t in range(kept):
                gathers.append(remote(half.at[at(d + t)], held.at[d - 1, t], d - 1, t, (at(d), blk)))
                gathers[-1].start()
        add(lambda t: half[at(t)], True)
        for d in range(1, na):
            for t in range(kept):
                gathers[(d - 1) * kept + t].wait_recv()
            add(lambda t: held[d - 1, t], False)
    eps_load.wait()

    swap = pltpu.make_async_remote_copy(
        src_ref=part.at[1 - core], dst_ref=core_in, send_sem=c_send, recv_sem=c_recv,
        device_id=(me, 2 * zed + 1 - core), device_id_type=MESH)
    swap.start()
    swap.wait_recv()
    sends = []
    for d in range(1, nz):
        to = lax.rem(zed + d, nz)
        out_z[d - 1] = (part[core, to] + core_in[to]).astype(jnp.bfloat16)
        sends.append(pltpu.make_async_remote_copy(
            src_ref=out_z.at[d - 1], dst_ref=in_z.at[d - 1], send_sem=z_send.at[d - 1],
            recv_sem=z_recv.at[d - 1], device_id=z_peer(d), device_id_type=MESH))
        sends[-1].start()
    total = part[core, zed] + core_in[zed]
    for d in range(1, nz):
        sends[d - 1].wait_recv()
        total = total + in_z[d - 1].astype(jnp.float32)

    pieces = [total[:, t * vir:(t + 1) * vir] for t in range(kept)]
    stacked = pieces
    if kept * rows < LANES:
        stacked = pieces + [jnp.zeros((LANES - kept * rows, vir), jnp.float32)]
    flat = jnp.transpose(jnp.concatenate(stacked, axis=0))
    turned[...] = flat
    lane = lax.broadcasted_iota(jnp.int32, (rows, LANES), 1)
    lane_e = lax.broadcasted_iota(jnp.int32, (8, LANES), 1)
    per = LANES // rows
    bands = rows // 8

    def rolled(value, shift):
        shift = shift % LANES
        return pltpu.roll(value, shift, 1) if shift else value

    for u in range(1, rest + 1):
        for k in range(nb):
            packed = jnp.zeros((8, LANES), jnp.float32)
            for q in range(bands):
                band = flat[k * rows + 8 * q:k * rows + 8 * q + 8]
                packed = jnp.where(lax.div(lane_e, rows) == q, rolled(band, rows * (q - u)), packed)
            packs[u - 1, k] = packed
    tails = []
    for u in range(1, rest + 1):
        for d in range(nb):
            to = lax.rem(blk + d, nb)
            tails.append(pltpu.make_async_remote_copy(
                src_ref=packs.at[u - 1, to], dst_ref=tail.at[u - 1, blk],
                send_sem=n_send.at[u - 1, d], recv_sem=n_recv.at[u - 1, d],
                device_id=(at(u), to), device_id_type=MESH))
            tails[-1].start()
    swaps = []
    for d in range(1, nb):
        to = lax.rem(blk + d, nb)
        swaps.append(pltpu.make_async_remote_copy(
            src_ref=turned.at[pl.ds(pl.multiple_of(to * rows, rows), rows)], dst_ref=tiles.at[blk],
            send_sem=t_send.at[d - 1], recv_sem=t_recv.at[d - 1],
            device_id=blk_peer(d), device_id_type=MESH))
        swaps[-1].start()
    tiles[blk] = turned[pl.ds(pl.multiple_of(blk * rows, rows), rows), :]

    level = eps_ref[...]
    turn = jnp.transpose(jnp.broadcast_to(level, (LANES, vir)))
    own_level = eps_buf[index_ref[me]]
    column = jnp.zeros((rows, LANES), jnp.float32)
    for k in range(nb):
        column = jnp.where(blk == k, turn[k * rows:(k + 1) * rows], column)
    column = column[:, :1]
    def ratio_of(t, piece):
        return piece / (((own_level + eps_buf[index_ref[at(t)]]) - column) - level)

    ratios = [ratio_of(t, pieces[t]) for t in range(kept)]
    scores = [ratios[t] * pieces[t] * 2.0 for t in range(kept)]
    for c in swaps:
        c.wait_recv()
    energy = jnp.zeros((8, LANES), jnp.float32)
    for t in range(kept):
        groups = []
        for g in range(vir // LANES):
            crossed = jnp.zeros((rows, LANES), jnp.float32)
            for m in range(per):
                crossed = jnp.where(lax.div(lane, rows) == m, rolled(tiles[g * per + m], rows * (m - t)), crossed)
            groups.append(crossed)
        crossed = jnp.concatenate(groups, axis=1)
        value = jnp.sum(scores[t] - ratios[t] * crossed)
        energy = jnp.where(lane_e == t, value, energy)
    e_own[...] = energy
    e_all[blk] = energy
    e_sends = []
    for d in range(1, nb):
        e_sends.append(pltpu.make_async_remote_copy(
            src_ref=e_own, dst_ref=e_all.at[blk], send_sem=e_send.at[d - 1], recv_sem=e_recv.at[d - 1],
            device_id=blk_peer(d), device_id_type=MESH))
        e_sends[-1].start()
    for u in range(1, rest + 1):
        for d in range(nb):
            e_sends.append(pltpu.make_async_remote_copy(
                src_ref=e_own, dst_ref=e_tail.at[u - 1, blk],
                send_sem=f_send.at[u - 1, d], recv_sem=f_recv.at[u - 1, d],
                device_id=(at(u), lax.rem(blk + d, nb)), device_id_type=MESH))
            e_sends[-1].start()

    for c in tails:
        c.wait_recv()
    for u in range(rest, 0, -1):
        groups = []
        for g in range(vir // LANES):
            strips = []
            for q in range(bands):
                strip = jnp.zeros((8, LANES), jnp.float32)
                for m in range(per):
                    moved = rolled(tail[u - 1, g * per + m], rows * (m - q))
                    strip = jnp.where(lax.div(lane_e, rows) == m, moved, strip)
                strips.append(strip)
            groups.append(jnp.concatenate(strips, axis=0))
        ratios.append(ratio_of(na - u, jnp.concatenate(groups, axis=1)))
    for j in range(na):
        chosen = ratios[0]
        for t in range(1, na):
            chosen = jnp.where(at(t) == j, ratios[t], chosen)
        amp_ref[0, :, j, :] = chosen

    for c in e_sends:
        c.wait_recv()
    sums = [e_all[...]] + [e_tail[u - 1] for u in range(1, rest + 1)]
    totals = []
    for group in sums:
        result = group[0]
        for k in range(1, nb):
            result = result + group[k]
        totals.append(result)
    final = jnp.zeros((8, LANES), jnp.float32)
    for t in range(na):
        group, place = (totals[0], t) if t < kept else (totals[na - t], na - t)
        value = jnp.sum(jnp.where(lane_e == place, group, 0.0)[:1], axis=1, keepdims=True)
        final = jnp.where(lane_e == at(t), value, final)
    e_ref[...] = final[:1, :na]
    for c in gathers + [swap] + sends + swaps + tails + e_sends:
        c.wait_send()


def body(three_center, slot_block, slot_aux, live_slots, vir_coef, eps_occ, eps_vir, occ_index):
    na = lax.axis_size("aux")
    nb = lax.axis_size("blk")
    nz = nb // 2
    slots, occ, aux_rows, span = three_center.shape
    vir = vir_coef.shape[1]
    depth = AUX_BLOCKS_DEV * aux_rows
    kept = na // 2 + 1
    rest = na - kept
    wide = kept * vir
    rows = vir // nb
    smem = pl.BlockSpec(memory_space=pltpu.SMEM)
    vmem = pl.BlockSpec(memory_space=pltpu.VMEM)
    anyspace = pl.BlockSpec(memory_space=pltpu.HBM)
    blocks = vir_coef.shape[0] // span
    chunks = max(n for n in range(1, 9) if blocks % n == 0)
    dma = pltpu.SemaphoreType.DMA
    return pl.pallas_call(
        functools.partial(pair_kernel, na, nb, slots),
        out_shape=(jax.ShapeDtypeStruct((1, rows, occ, vir), jnp.float32),
                   jax.ShapeDtypeStruct((1, na), jnp.float32)),
        in_specs=[smem] * 4 + [anyspace] * 3 + [vmem],
        out_specs=(vmem, vmem),
        scratch_shapes=[
            pltpu.VMEM((slots, occ, aux_rows, span), jnp.bfloat16),
            pltpu.VMEM((blocks, span, vir), jnp.bfloat16),
            pltpu.VMEM((slots * span, AUX_BLOCKS_DEV * vir), jnp.bfloat16),
            pltpu.SMEM((eps_occ.shape[0],), jnp.float32),
            pltpu.VMEM((occ, depth, vir), jnp.bfloat16),
            pltpu.VMEM((na - 1, kept, depth, vir), jnp.bfloat16),
            pltpu.VMEM((2, nz, rows, wide), jnp.float32),
            pltpu.VMEM((nz, rows, wide), jnp.float32),
            pltpu.VMEM((nz - 1, rows, wide), jnp.bfloat16),
            pltpu.VMEM((nz - 1, rows, wide), jnp.bfloat16),
            pltpu.VMEM((vir, LANES), jnp.float32),
            pltpu.VMEM((nb, rows, LANES), jnp.float32),
            pltpu.VMEM((rest, nb, 8, LANES), jnp.float32),
            pltpu.VMEM((rest, nb, 8, LANES), jnp.float32),
            pltpu.VMEM((8, LANES), jnp.float32),
            pltpu.VMEM((nb, 8, LANES), jnp.float32),
            pltpu.VMEM((rest, nb, 8, LANES), jnp.float32),
            dma((slots,)), dma((chunks,)), dma,
            dma((na - 1, kept + 1)), dma((na - 1, kept + 1)), dma, dma, dma((nz - 1,)), dma((nz - 1,)),
            dma((nb - 1,)), dma((nb - 1,)), dma((rest, nb)), dma((rest, nb)),
            dma((nb - 1,)), dma((nb - 1,)), dma((rest, nb)), dma((rest, nb)),
        ],
        compiler_params=pltpu.CompilerParams(collective_id=0, has_side_effects=True, vmem_limit_bytes=56000000),
    )(slot_block, slot_aux, live_slots, occ_index, three_center,
      vir_coef.reshape(blocks, span, vir), eps_occ, eps_vir.reshape(1, vir))


def solution(mesh):
    in_specs = (
        P(("aux", "blk"), None, None, None),
        P(("aux", "blk")),
        P(("aux", "blk")),
        P(("aux", "blk")),
        P(),
        P(),
        P(),
        P(),
    )
    out_specs = (P("aux", "blk", None, None), P("aux", None))
    return jax.shard_map(body, mesh=mesh, in_specs=in_specs, out_specs=out_specs, check_vma=False)
```
